32 devices in a mesh: row: 4 (over y, core), col: 8 (over z, x).
Axes of the slice: x: 2, y: 2, z: 4, core: 2. Of those that a mesh axis runs over, the one named last changes fastest.
Arguments:
- quant_acts: bfloat16 [1024, 8192], P('col', 'row'), may hold values from -6 to 6
- full_acts: bfloat16 [1024, 8192], P('col', 'row'), may hold values from -6 to 6
Outputs:
- hessian: float32 [8192, 8192], P('row', 'col')
- cross_term: float32 [8192, 8192], P('row', 'col')
The draws below stay inside these ranges and needn't reach their ends.
All inputs are finite; a program needn't handle non-finite values.
Results may differ from the reference program's by a relative error of at most 0.0028.
Values may be sent and summed in bfloat16 or wider, within the bound.
No kernel may reach another device: no remote copies, remote signals or barrier semaphores. Data moves between devices by JAX's collectives and lax.ppermute only.
A program may use at most 64 MiB of HBM per device.

```python
import jax
import jax.numpy as jnp

SLAB = 8192
TOKENS = 1024


def level_of(key, shape, pieces, low, top_value):
    def one(position, blocks):
        heights = jax.random.uniform(jax.random.fold_in(jax.random.fold_in(key, 6), position), (blocks,), jnp.float32, low / len(pieces), top_value / len(pieces))
        return jnp.repeat(jnp.exp(heights), shape[position] // blocks).reshape((-1,) + (1,) * (len(shape) - position - 1))

    gain = one(*pieces[0])
    for cut in pieces[1:]:
        gain = gain * one(*cut)
    return gain


def scatter_about(key, shape, scale, bound, split=(), dtype=jnp.bfloat16):
    factor_of = level_of(key, shape, split, -0.22, 0.18) if split else 1.0
    result = jax.random.normal(key, shape, jnp.float32) * scale * factor_of
    return jnp.minimum(jnp.maximum(result, -bound), bound).astype(dtype)


def setup_inputs(seed: int = 0) -> dict:
    splits = jax.random.split(jax.random.key(seed), 3)
    quant_acts = scatter_about(splits[0], (TOKENS, SLAB), 1.0, 6.0, ((0, 8), (1, 4)))
    full_acts = scatter_about(splits[1], (TOKENS, SLAB), 1.0, 6.0, ((0, 8), (1, 4)))
    return {"quant_acts": quant_acts, "full_acts": full_acts}


def reference(quant_acts, full_acts):
    deltas = (full_acts.astype(jnp.float32) - quant_acts.astype(jnp.float32)).astype(jnp.bfloat16)
    scale = 1.0 / TOKENS
    hessian = jnp.dot(quant_acts.T, quant_acts, preferred_element_type=jnp.float32) * scale
    cross_term = jnp.dot(deltas.T, quant_acts, preferred_element_type=jnp.float32) * scale
    return hessian, cross_term
```

```python
import functools

import jax
import jax.numpy as jnp
from jax import lax
from jax.experimental import pallas as pl
from jax.experimental.pallas import tpu as pltpu
from jax.sharding import PartitionSpec as P


def ring_of(size):
    order = list(range(0, size, 2)) + list(range(size - 1, 0, -2))
    forth = [(order[i], order[(i + 1) % size]) for i in range(size)]
    return forth, [(b, a) for a, b in forth]


def product_kernel(pieces, groups, scale, *refs):
    left, right = refs[:pieces], refs[pieces : pieces + groups]
    out, left_all, right_all = refs[-3:]

    @pl.when(pl.program_id(0) == 0)
    def _():
        at = 0
        for ref in right:
            right_all[at : at + ref.shape[0], :] = ref[...]
            at += ref.shape[0]

    at = 0
    for ref in left:
        left_all[at : at + ref.shape[0], :] = ref[...]
        at += ref.shape[0]
    out[...] = scale * lax.dot_general(
        left_all[...], right_all[...], (((0,), (0,)), ((), ())), preferred_element_type=jnp.float32
    )


def product(left, right, scale, tile, total_rows, first_row=0, into=None, after=()):
    depth = sum(p.shape[0] for p in left)
    rows, columns = left[0].shape[1], right[0].shape[1]
    tile = min(tile, rows)
    first_tile = first_row // tile
    extra = list(after) + ([into] if into is not None else [])
    return pl.pallas_call(
        functools.partial(product_kernel, len(left), len(right), scale),
        grid=(rows // tile,),
        in_specs=[pl.BlockSpec((p.shape[0], tile), lambda i: (0, i)) for p in left]
        + [pl.BlockSpec(p.shape, lambda i: (0, 0), pipeline_mode=pl.Buffered(1)) for p in right]
        + [pl.BlockSpec(memory_space=pl.ANY) for _ in extra],
        out_specs=pl.BlockSpec((tile, columns), lambda i: (i + first_tile, 0)),
        out_shape=jax.ShapeDtypeStruct((total_rows, columns), jnp.float32),
        input_output_aliases={} if into is None else {len(left) + len(right) + len(extra) - 1: 0},
        scratch_shapes=[
            pltpu.VMEM((depth, tile), jnp.bfloat16),
            pltpu.VMEM((depth, columns), jnp.bfloat16),
        ],
        cost_estimate=pl.CostEstimate(
            flops=2 * rows * columns * depth,
            bytes_accessed=2 * depth * (rows + columns) + 4 * rows * columns,
            transcendentals=0,
        ),
    )(*left, *right, *extra)


def ring_gather(own, size, forth, back):
    pieces = [own]
    ahead = behind = own
    for step in range(1, size // 2):
        ahead = lax.ppermute(ahead, "col", forth)
        behind = lax.ppermute(behind, "col", back)
        pieces += [ahead, behind]
    half = own.shape[0] // 2
    pieces.append(lax.ppermute(ahead[:half], "col", forth))
    pieces.append(lax.ppermute(behind[half:], "col", back))
    return pieces


def local(rows_count, size, quant_acts, full_acts):
    forth, back = ring_of(size)
    features = quant_acts.shape[1]
    column = lax.axis_index("col")
    row = lax.axis_index("row")
    per = size // rows_count
    source = column // per
    part = column % per
    width = features // per

    def columns_of(x):
        chosen = x[:, :width]
        for j in range(1, per):
            chosen = jnp.where(part == j, x[:, j * width : (j + 1) * width], chosen)
        return chosen

    def spread(block):
        bit = rows_count // 2
        covered = [0]
        while bit:
            pairs = []
            for c in range(size):
                for offset in covered:
                    at = (c // per) ^ offset
                    pairs.append((at * size + c, (at ^ bit) * size + c))
            came = lax.ppermute(block, ("row", "col"), pairs)
            fresh = [o ^ bit for o in covered]
            relation = row ^ source
            got = functools.reduce(jnp.logical_or, [relation == o for o in fresh])
            block = jnp.where(got, came, block)
            covered += fresh
            bit //= 2
        return block

    deltas = (full_acts.astype(jnp.float32) - quant_acts.astype(jnp.float32)).astype(jnp.bfloat16)
    quant = ring_gather(quant_acts, size, forth, back)
    total_tokens = sum(p.shape[0] for p in quant)
    half = features // 2
    first = ring_gather(deltas[:, :half], size, forth, back)
    second = ring_gather(deltas[:, half:], size, forth, back)
    cuts = (0, 5, 7, len(quant))
    right = [
        spread(jnp.concatenate([columns_of(q) for q in quant[a:b]]))
        for a, b in zip(cuts[:-1], cuts[1:])
    ]
    scale = 1.0 / total_tokens
    hessian = product(quant, right, scale, 256, features)
    cross_term = product(first, right, scale, 256, features, after=(hessian,))
    cross_term = product(second, right, scale, 256, features, half, cross_term)
    return hessian, cross_term


def solution(mesh):
    return jax.shard_map(
        functools.partial(local, mesh.shape["row"], mesh.shape["col"]),
        mesh=mesh,
        in_specs=(P("col", "row"), P("col", "row")),
        out_specs=(P("row", "col"), P("row", "col")),
        check_vma=False,
    )
```
